1024 devices in a mesh: replica: 32 (over x_hi, z), expert: 32 (over x_lo, y, core).
Axes of the slice: x: 8 (x_hi: 4, x_lo: 2; x = x_hi * 2 + x_lo), y: 8, z: 8, core: 2. Of those that a mesh axis runs over, the one named last changes fastest.
Arguments:
- master: float32 [32, 32, 32, 2, 768], P('replica', 'expert'), may hold values from -6 to 6
- first_moment: float32 [32, 32, 32, 2, 768], P('replica', 'expert'), may hold values from -4 to 4
- second_moment: float32 [32, 32, 32, 2, 768], P('replica', 'expert'), may hold values from 0.001 to 1
- gradient: bfloat16 [32, 32, 32, 2, 768], P('replica', 'expert'), may hold values from -6 to 6
- scale_exponent: int32 [32, 32, 32, 2, 6], P('replica', 'expert'), may hold values from 3 to 7
- slot_expert: int32 [32, 32, 32], P('replica', 'expert'), may hold values from 0 to 31, each once within a row
- expert_owner: int32 [32], replicated, may hold values from 0 to 31, each once
- serving_weights: bfloat16 [32, 2048, 768], P('expert'), may hold values from -6 to 6
Outputs:
- master_out: float32 [32, 32, 32, 2, 768], P('replica', 'expert')
- first_out: float32 [32, 32, 32, 2, 768], P('replica', 'expert')
- second_out: float32 [32, 32, 32, 2, 768], P('replica', 'expert')
- serving_out: bfloat16 [32, 2048, 768], P('expert')
The draws below stay inside these ranges and needn't reach their ends.
Inputs may be any that keep to these rules, and one draw needn't show every extreme that they name: `slot_expert`: each row along the last dimension names every expert once. `expert_owner`: names every owner once.
All inputs are finite; a program needn't handle non-finite values.
Results may differ from the reference program's by a relative error of at most 0.0015.
Values may be sent and summed in bfloat16 or wider, within the bound.
No kernel may reach another device: no remote copies, remote signals or barrier semaphores. Data moves between devices by JAX's collectives and lax.ppermute only.
A program may use at most 64 MiB of HBM per device.

```python
import math
import jax
import jax.numpy as jnp

D_WIN = 2048
F_WIN = 768
BLOCK = 128
EXPERTS = 32
SUB_ROWS = 2
NBLK = 6
N_REPLICA = 32
N_EXPERT = 32


def place_ends(entries, rng, least, high):
    longest = entries.shape.index(max(entries.shape))
    spots = []
    for shift in (0, 1):
        where = [jax.random.randint(jax.random.fold_in(rng, axis), (), 0, length) for axis, length in enumerate(entries.shape)]
        where[longest] = (where[longest] + shift) % entries.shape[longest]
        spots.append(tuple(where))
    return entries.at[spots[0]].set(least).at[spots[1]].set(high)


def levels(rng, shape, cuts, low, high):
    factor_of, own = 1.0, jax.random.fold_in(rng, 6)
    for position, shards_of in cuts:
        steps = jnp.exp(jax.random.uniform(jax.random.fold_in(own, position), (shards_of,), jnp.float32, low / len(cuts), high / len(cuts)))
        factor_of = factor_of * jnp.repeat(steps, shape[position] // shards_of).reshape([-1 if axis == position else 1 for axis in range(len(shape))])
    return factor_of


def bell_draw(stream_key, shape, scale, reach, shards=(), held_as=jnp.bfloat16):
    loudness = levels(stream_key, shape, shards, -0.22, 0.18) if shards else 1.0
    result = jax.random.normal(stream_key, shape, jnp.float32) * scale * loudness
    return jnp.minimum(jnp.maximum(result, -reach), reach).astype(held_as)


def setup_inputs(seed: int = 0) -> dict:
    key_of = jax.random.split(jax.random.key(seed), 9)
    return {
        "master": bell_draw(key_of[0], (N_REPLICA, N_EXPERT, EXPERTS, SUB_ROWS, F_WIN), 1.0, 6.0, ((0, 32), (1, 32)), jnp.float32),
        "first_moment": bell_draw(key_of[1], (N_REPLICA, N_EXPERT, EXPERTS, SUB_ROWS, F_WIN), 0.3, 4.0, ((0, 32), (1, 32)), jnp.float32),
        "second_moment": jnp.clip(jnp.exp(math.log(1.0) - 6.9077552 * jax.random.uniform(key_of[2], (N_REPLICA, N_EXPERT, EXPERTS, SUB_ROWS, F_WIN), jnp.float32) ** levels(key_of[2], (N_REPLICA, N_EXPERT, EXPERTS, SUB_ROWS, F_WIN), ((0, 32), (1, 32)), -0.2, 0.2)), 0.001, 1.0),
        "gradient": bell_draw(key_of[3], (N_REPLICA, N_EXPERT, EXPERTS, SUB_ROWS, F_WIN), 1.0, 6.0, ((0, 32), (1, 32))),
        "scale_exponent": place_ends(jax.random.randint(key_of[4], (N_REPLICA, N_EXPERT, EXPERTS, SUB_ROWS, NBLK), 3, 8), jax.random.fold_in(key_of[4], 1), 3, 7).astype(jnp.int32),
        "slot_expert": jax.vmap(lambda own: jax.random.permutation(own, EXPERTS))(jax.random.split(key_of[5], N_REPLICA * N_EXPERT)).reshape((N_REPLICA, N_EXPERT, EXPERTS)).astype(jnp.int32),
        "expert_owner": jax.random.permutation(key_of[6], EXPERTS).astype(jnp.int32),
        "serving_weights": bell_draw(key_of[7], (EXPERTS, D_WIN, F_WIN), 1.0, 6.0, ((0, 32),)),
    }


def reference(master, first_moment, second_moment, gradient, scale_exponent, slot_expert, expert_owner, serving_weights):
    grad_full = gradient.astype(jnp.float32)
    first_out = 0.9 * first_moment + 0.1 * grad_full
    second_out = 0.95 * second_moment + 0.05 * grad_full * grad_full
    corr_first = 1.0 - 0.9 ** 10
    corr_second = 1.0 - 0.95 ** 10
    update = first_out / corr_first / (jnp.sqrt(second_out / corr_second) + 1e-08) + 0.1 * master
    delta = -0.1 * update
    master_out = master + delta
    scale = jnp.exp2(-scale_exponent.astype(jnp.float32))
    shaped = delta.reshape(delta.shape[:-1] + (NBLK, BLOCK))
    coded = jnp.clip(shaped / scale[..., None], -8.0, 8.0).astype(jnp.bfloat16)
    inverse = jnp.argsort(slot_expert, axis=-1).astype(jnp.int32)
    coded_by = jnp.take_along_axis(coded, inverse[:, :, :, None, None, None], axis=2)
    scale_by = jnp.take_along_axis(scale, inverse[:, :, :, None, None], axis=2)
    coded_by = jnp.transpose(coded_by, (2, 0, 1, 3, 4, 5)).reshape(EXPERTS, D_WIN, NBLK, BLOCK)
    scale_by = jnp.transpose(scale_by, (2, 0, 1, 3, 4)).reshape(EXPERTS, D_WIN, NBLK)
    served = jnp.argsort(expert_owner).astype(jnp.int32)
    coded_own = coded_by[served]
    scale_own = scale_by[served]
    added = coded_own.astype(jnp.float32) * scale_own[..., None]
    serving_out = (serving_weights.astype(jnp.float32) + added.reshape(EXPERTS, D_WIN, F_WIN)).astype(jnp.bfloat16)
    return (master_out, first_out, second_out, serving_out)
```

```python
import jax
import jax.numpy as jnp
from jax import lax
from jax.sharding import PartitionSpec as P


def shards(
    master,
    first_moment,
    second_moment,
    gradient,
    scale_exponent,
    slot_expert,
    expert_owner,
    serving_weights,
):
    grad_full = gradient.astype(jnp.float32)
    first_out = 0.9 * first_moment + 0.1 * grad_full
    second_out = 0.95 * second_moment + 0.05 * grad_full * grad_full
    corr_first = 1.0 - 0.9**10
    corr_second = 1.0 - 0.95**10
    update = first_out / corr_first / (jnp.sqrt(second_out / corr_second) + 1e-08) + 0.1 * master
    delta = -0.1 * update
    master_out = master + delta
    slots = master.shape[2]
    sub_rows = master.shape[3]
    columns = master.shape[4]
    blocks = scale_exponent.shape[4]
    limit = 8.0 * jnp.exp2(-scale_exponent[0, 0].astype(jnp.float32))
    shaped = delta[0, 0].reshape(slots, sub_rows, blocks, columns // blocks)
    added = (
        jnp.clip(shaped, -limit[..., None], limit[..., None])
        .astype(jnp.bfloat16)
        .reshape(slots, sub_rows, columns)
    )
    target = expert_owner[slot_expert[0, 0]]
    ordering = jnp.zeros((slots,), jnp.int32).at[target].set(jnp.arange(slots, dtype=jnp.int32))
    added_recv = lax.all_to_all(added[ordering], "expert", split_axis=0, concat_axis=0, tiled=True)
    piece = added_recv.reshape(slots * sub_rows, columns)
    gathered = lax.all_gather(piece, "replica", axis=0, tiled=True)
    new_rows = (serving_weights[0].astype(jnp.float32) + gathered.astype(jnp.float32)).astype(jnp.bfloat16)
    return (master_out, first_out, second_out, new_rows[None])


def solution(mesh):
    in_specs = (
        P("replica", "expert", None, None, None),
        P("replica", "expert", None, None, None),
        P("replica", "expert", None, None, None),
        P("replica", "expert", None, None, None),
        P("replica", "expert", None, None, None),
        P("replica", "expert", None),
        P(),
        P("expert", None, None),
    )
    out_specs = (
        P("replica", "expert", None, None, None),
        P("replica", "expert", None, None, None),
        P("replica", "expert", None, None, None),
        P("expert", None, None),
    )
    return jax.shard_map(shards, mesh=mesh, in_specs=in_specs, out_specs=out_specs, check_vma=False)
```

```python
import jax
import jax.numpy as jnp
from jax import lax
from jax.sharding import PartitionSpec as P

RING = 8
LIFT = 2.0**15


def shards(
    master,
    first_moment,
    second_moment,
    gradient,
    scale_exponent,
    slot_expert,
    expert_owner,
    serving_weights,
):
    grad_full = gradient.astype(jnp.float32)
    first_out = 0.9 * first_moment + 0.1 * grad_full
    second_out = 0.95 * second_moment + 0.05 * grad_full * grad_full
    corr_first = 1.0 - 0.9**10
    corr_second = 1.0 - 0.95**10
    update = first_out / corr_first / (jnp.sqrt(second_out / corr_second) + 1e-08) + 0.1 * master
    delta = -0.1 * update
    master_out = master + delta
    slots = master.shape[2]
    sub_rows = master.shape[3]
    columns = master.shape[4]
    blocks = scale_exponent.shape[4]
    limit = 8.0 * jnp.exp2(-scale_exponent[0, 0].astype(jnp.float32))
    shaped = delta[0, 0].reshape(slots, sub_rows, blocks, columns // blocks)
    added = (
        jnp.clip(shaped, -limit[..., None], limit[..., None])
        .astype(jnp.bfloat16)
        .reshape(slots, sub_rows, columns)
    )
    target = expert_owner[slot_expert[0, 0]]
    ordering = jnp.zeros((slots,), jnp.int32).at[target].set(jnp.arange(slots, dtype=jnp.int32))
    added_recv = lax.all_to_all(added[ordering], "expert", split_axis=0, concat_axis=0, tiled=True)
    piece = added_recv.reshape(slots * sub_rows, columns)
    replicas = lax.axis_size("replica")
    along_x = [[x * RING + z for x in range(replicas // RING)] for z in range(RING)]
    along_z = [[x * RING + z for z in range(RING)] for x in range(replicas // RING)]
    part = lax.all_gather(piece, "replica", axis=0, tiled=False, axis_index_groups=along_x)
    wire = (part.astype(jnp.float32) * LIFT).astype(jnp.float16)
    whole = lax.all_gather(wire, "replica", axis=0, tiled=False, axis_index_groups=along_z)
    gathered = whole.astype(jnp.float32) * (1.0 / LIFT)
    gathered = jnp.transpose(gathered, (1, 0, 2, 3)).reshape(serving_weights.shape[1:])
    new_rows = (serving_weights[0].astype(jnp.float32) + gathered).astype(jnp.bfloat16)
    return (master_out, first_out, second_out, new_rows[None])


def solution(mesh):
    in_specs = (
        P("replica", "expert", None, None, None),
        P("replica", "expert", None, None, None),
        P("replica", "expert", None, None, None),
        P("replica", "expert", None, None, None),
        P("replica", "expert", None, None, None),
        P("replica", "expert", None),
        P(),
        P("expert", None, None),
    )
    out_specs = (
        P("replica", "expert", None, None, None),
        P("replica", "expert", None, None, None),
        P("replica", "expert", None, None, None),
        P("expert", None, None),
    )
    return jax.shard_map(shards, mesh=mesh, in_specs=in_specs, out_specs=out_specs, check_vma=False)
```

```python
import jax
import jax.numpy as jnp
from jax import lax
from jax.experimental import pallas as pl
from jax.experimental.pallas import tpu as pltpu
from jax.sharding import Mesh
from jax.sharding import PartitionSpec as P

RING = 8
LIFT = 2.0**15
REPLICA = ("x_hi", "z")


def step_kernel(
    slot_ref,
    owner_ref,
    exponent_ref,
    master_ref,
    first_ref,
    second_ref,
    grad_ref,
    master_out_ref,
    first_out_ref,
    second_out_ref,
    sent_ref,
):
    slots, sub_rows, columns = master_ref.shape
    blocks = exponent_ref.shape[2]
    grad_full = grad_ref[...].astype(jnp.float32)
    first_out = 0.9 * first_ref[...] + 0.1 * grad_full
    second_out = 0.95 * second_ref[...] + 0.05 * grad_full * grad_full
    first_out_ref[...] = first_out
    second_out_ref[...] = second_out
    corr_first = 1.0 - 0.9**10
    corr_second = 1.0 - 0.95**10
    master = master_ref[...]
    update = first_out / corr_first / (jnp.sqrt(second_out / corr_second) + 1e-08) + 0.1 * master
    delta = -0.1 * update
    master_out_ref[...] = master + delta
    limit = 8.0 * jnp.exp2(-exponent_ref[...].astype(jnp.float32))
    width = columns // blocks
    limits = jnp.concatenate(
        [jnp.broadcast_to(limit[:, :, b : b + 1], (slots, sub_rows, width)) for b in range(blocks)],
        axis=2,
    )
    added = jnp.clip(delta, -limits, limits).astype(jnp.bfloat16)
    for slot in range(slots):
        owner = owner_ref[slot_ref[slot]]
        sent_ref[pl.ds(owner, 1)] = added[slot : slot + 1]


def shards(
    master,
    first_moment,
    second_moment,
    gradient,
    scale_exponent,
    slot_expert,
    expert_owner,
    serving_weights,
):
    state = jax.ShapeDtypeStruct(master.shape[2:], jnp.float32)
    wire_rows = jax.ShapeDtypeStruct(master.shape[2:], jnp.bfloat16)
    in_vmem = pl.BlockSpec(memory_space=pltpu.VMEM)
    in_smem = pl.BlockSpec(memory_space=pltpu.SMEM)
    master_out, first_out, second_out, sent = pl.pallas_call(
        step_kernel,
        in_specs=[in_smem, in_smem] + [in_vmem] * 5,
        out_specs=[in_vmem] * 4,
        out_shape=[state, state, state, wire_rows],
    )(
        slot_expert[0, 0],
        expert_owner,
        scale_exponent[0, 0],
        master[0, 0],
        first_moment[0, 0],
        second_moment[0, 0],
        gradient[0, 0],
    )
    received = lax.all_to_all(sent, "expert", split_axis=0, concat_axis=0, tiled=True)
    piece = received.reshape(-1, received.shape[2])
    part = lax.all_gather(piece, "x_hi", axis=0, tiled=False)
    wire = (part.astype(jnp.float32) * LIFT).astype(jnp.float16)
    whole = lax.all_gather(wire, "z", axis=1, tiled=True)
    serving = serving_weights.reshape(whole.shape)
    added = whole.astype(jnp.float32) * (1.0 / LIFT)
    new_rows = (serving.astype(jnp.float32) + added).astype(jnp.bfloat16)
    serving_out = new_rows.reshape(serving_weights.shape)
    return (master_out[None, None], first_out[None, None], second_out[None, None], serving_out)


def solution(mesh):
    replicas, experts = mesh.devices.shape
    split = Mesh(mesh.devices.reshape(replicas // RING, RING, experts), (*REPLICA, "expert"))
    flat = P(REPLICA, "expert", None, None, None)
    served = P("expert", None, None)
    in_specs = (flat, flat, flat, flat, flat, P(REPLICA, "expert", None), P(), served)
    out_specs = (flat, flat, flat, served)
    return jax.shard_map(shards, mesh=split, in_specs=in_specs, out_specs=out_specs, check_vma=False)
```

```python
import jax
import jax.numpy as jnp
from jax import lax
from jax.experimental import pallas as pl
from jax.experimental.pallas import tpu as pltpu
from jax.sharding import Mesh
from jax.sharding import PartitionSpec as P

RING = 8
CORES = 2
LIFT = 2.0**15
REPLICA = ("x_hi", "z")
EXPERT = ("tile", "core")


def step_kernel(
    slot_ref,
    owner_ref,
    exponent_ref,
    master_ref,
    first_ref,
    second_ref,
    grad_ref,
    master_out_ref,
    first_out_ref,
    second_out_ref,
    sent_ref,
):
    slots, sub_rows, columns = master_ref.shape
    blocks = exponent_ref.shape[0]
    grad_full = grad_ref[...].astype(jnp.float32)
    first_out = 0.9 * first_ref[...] + 0.1 * grad_full
    second_out = 0.95 * second_ref[...] + 0.05 * grad_full * grad_full
    first_out_ref[...] = first_out
    second_out_ref[...] = second_out
    corr_first = 1.0 - 0.9**10
    corr_second = 1.0 - 0.95**10
    master = master_ref[...]
    update = first_out / corr_first / (jnp.sqrt(second_out / corr_second) + 1e-08) + 0.1 * master
    delta = -0.1 * update
    master_out_ref[...] = master + delta
    limit = 8.0 * jnp.exp2(-exponent_ref[...].astype(jnp.float32))
    width = columns // blocks
    for slot in range(slots):
        limits = jnp.concatenate(
            [
                jnp.broadcast_to(limit[b, :, slot : slot + 1], (sub_rows, width))
                for b in range(blocks)
            ],
            axis=1,
        )
        added = jnp.clip(delta[slot], -limits, limits).astype(jnp.bfloat16)
        owner = owner_ref[slot_ref[slot]]
        place = lax.rem(owner, CORES) * (slots // CORES) + lax.div(owner, CORES)
        sent_ref[pl.ds(place, 1)] = added[None]


def shards(
    master,
    first_moment,
    second_moment,
    gradient,
    scale_exponent,
    slot_expert,
    expert_owner,
    serving_weights,
):
    slots, sub_rows, columns = master.shape[2:]
    state = jax.ShapeDtypeStruct((slots, sub_rows, columns), jnp.float32)
    wire_rows = jax.ShapeDtypeStruct((slots, sub_rows, columns), jnp.bfloat16)
    in_vmem = pl.BlockSpec(memory_space=pltpu.VMEM)
    in_smem = pl.BlockSpec(memory_space=pltpu.SMEM)
    master_out, first_out, second_out, sent = pl.pallas_call(
        step_kernel,
        in_specs=[in_smem, in_smem] + [in_vmem] * 5,
        out_specs=[in_vmem] * 4,
        out_shape=[state, state, state, wire_rows],
    )(
        slot_expert[0, 0],
        expert_owner,
        jnp.transpose(scale_exponent[0, 0], (2, 1, 0)),
        master[0, 0],
        first_moment[0, 0],
        second_moment[0, 0],
        gradient[0, 0],
    )
    on_core = lax.all_to_all(sent, "core", split_axis=0, concat_axis=0, tiled=True)
    tiles = slots // CORES
    by_tile = jnp.transpose(on_core.reshape(CORES, tiles, sub_rows, columns), (1, 0, 2, 3))
    copies = lax.axis_size("x_hi")
    blocks = jnp.broadcast_to(
        by_tile.reshape(1, tiles, CORES * sub_rows, columns),
        (copies, tiles, CORES * sub_rows, columns),
    ).reshape(copies * tiles, CORES * sub_rows, columns)
    received = lax.all_to_all(blocks, ("x_hi", "tile"), split_axis=0, concat_axis=0, tiled=True)
    part = received.reshape(copies, slots * sub_rows, columns)
    wire = (part.astype(jnp.float32) * LIFT).astype(jnp.float16)
    whole = lax.all_gather(wire, "z", axis=1, tiled=True)
    serving = serving_weights.reshape(whole.shape)
    added = whole.astype(jnp.float32) * (1.0 / LIFT)
    new_rows = (serving.astype(jnp.float32) + added).astype(jnp.bfloat16)
    serving_out = new_rows.reshape(serving_weights.shape)
    return (master_out[None, None], first_out[None, None], second_out[None, None], serving_out)


def solution(mesh):
    replicas, experts = mesh.devices.shape
    shape = (replicas // RING, RING, experts // CORES, CORES)
    split = Mesh(mesh.devices.reshape(shape), (*REPLICA, *EXPERT))
    flat = P(REPLICA, EXPERT, None, None, None)
    served = P(EXPERT, None, None)
    in_specs = (flat, flat, flat, flat, flat, P(REPLICA, EXPERT, None), P(), served)
    out_specs = (flat, flat, flat, served)
    return jax.shard_map(shards, mesh=split, in_specs=in_specs, out_specs=out_specs, check_vma=False)
```

```python
import jax
import jax.numpy as jnp
from jax import lax
from jax.experimental import pallas as pl
from jax.experimental.pallas import tpu as pltpu
from jax.sharding import Mesh
from jax.sharding import PartitionSpec as P

RING = 8
LIFT = 2.0**15
REPLICA = ("x_hi", "z")


def step_kernel(
    slot_ref,
    owner_ref,
    exponent_ref,
    master_ref,
    first_ref,
    second_ref,
    grad_ref,
    master_out_ref,
    first_out_ref,
    second_out_ref,
    sent_ref,
):
    slots, sub_rows, columns = master_ref.shape
    blocks = exponent_ref.shape[0]
    grad_full = grad_ref[...].astype(jnp.float32)
    first_out = 0.9 * first_ref[...] + 0.1 * grad_full
    second_out = 0.95 * second_ref[...] + 0.05 * grad_full * grad_full
    first_out_ref[...] = first_out
    second_out_ref[...] = second_out
    corr_first = 1.0 - 0.9**10
    corr_second = 1.0 - 0.95**10
    master = master_ref[...]
    update = first_out / corr_first / (jnp.sqrt(second_out / corr_second) + 1e-08) + 0.1 * master
    delta = -0.1 * update
    master_out_ref[...] = master + delta
    limit = 8.0 * jnp.exp2(-exponent_ref[...].astype(jnp.float32))
    width = columns // blocks
    for slot in range(slots):
        limits = jnp.concatenate(
            [
                jnp.broadcast_to(limit[b, :, slot : slot + 1], (sub_rows, width))
                for b in range(blocks)
            ],
            axis=1,
        )
        added = jnp.clip(delta[slot], -limits, limits).astype(jnp.bfloat16)
        sent_ref[pl.ds(owner_ref[slot_ref[slot]], 1)] = added[None]


def shards(
    master,
    first_moment,
    second_moment,
    gradient,
    scale_exponent,
    slot_expert,
    expert_owner,
    serving_weights,
):
    state = jax.ShapeDtypeStruct(master.shape[2:], jnp.float32)
    wire_rows = jax.ShapeDtypeStruct(master.shape[2:], jnp.bfloat16)
    in_vmem = pl.BlockSpec(memory_space=pltpu.VMEM)
    in_smem = pl.BlockSpec(memory_space=pltpu.SMEM)
    master_out, first_out, second_out, sent = pl.pallas_call(
        step_kernel,
        in_specs=[in_smem, in_smem] + [in_vmem] * 5,
        out_specs=[in_vmem] * 4,
        out_shape=[state, state, state, wire_rows],
    )(
        slot_expert[0, 0],
        expert_owner,
        jnp.transpose(scale_exponent[0, 0], (2, 1, 0)),
        master[0, 0],
        first_moment[0, 0],
        second_moment[0, 0],
        gradient[0, 0],
    )
    received = lax.all_to_all(sent, "expert", split_axis=0, concat_axis=0, tiled=True)
    piece = received.reshape(-1, received.shape[2])
    part = lax.all_gather(piece, "x_hi", axis=0, tiled=False)
    wire = (part.astype(jnp.float32) * LIFT).astype(jnp.float16)
    whole = lax.all_gather(wire, "z", axis=1, tiled=True)
    serving = serving_weights.reshape(whole.shape)
    added = whole.astype(jnp.float32) * (1.0 / LIFT)
    new_rows = (serving.astype(jnp.float32) + added).astype(jnp.bfloat16)
    serving_out = new_rows.reshape(serving_weights.shape)
    return (master_out[None, None], first_out[None, None], second_out[None, None], serving_out)


def solution(mesh):
    replicas, experts = mesh.devices.shape
    split = Mesh(mesh.devices.reshape(replicas // RING, RING, experts), (*REPLICA, "expert"))
    flat = P(REPLICA, "expert", None, None, None)
    served = P("expert", None, None)
    in_specs = (flat, flat, flat, flat, flat, P(REPLICA, "expert", None), P(), served)
    out_specs = (flat, flat, flat, served)
    return jax.shard_map(shards, mesh=split, in_specs=in_specs, out_specs=out_specs, check_vma=False)
```

```python
import jax
import jax.numpy as jnp
from jax import lax
from jax.experimental import pallas as pl
from jax.experimental.pallas import tpu as pltpu
from jax.sharding import Mesh
from jax.sharding import PartitionSpec as P

RING = 8
LIFT = 2.0**15
REPLICA = ("x_hi", "z")


def adamw(master, first_moment, second_moment, gradient):
    grad_full = gradient.astype(jnp.float32)
    first_out = 0.9 * first_moment + 0.1 * grad_full
    second_out = 0.95 * second_moment + 0.05 * grad_full * grad_full
    corr_first = 1.0 - 0.9**10
    corr_second = 1.0 - 0.95**10
    update = first_out / corr_first / (jnp.sqrt(second_out / corr_second) + 1e-08) + 0.1 * master
    return first_out, second_out, -0.1 * update


def coded_kernel(
    slot_ref,
    owner_ref,
    exponent_ref,
    master_ref,
    first_ref,
    second_ref,
    grad_ref,
    sent_ref,
):
    slots, sub_rows, columns = master_ref.shape
    blocks = exponent_ref.shape[0]
    _, _, delta = adamw(master_ref[...], first_ref[...], second_ref[...], grad_ref[...])
    limit = 8.0 * jnp.exp2(-exponent_ref[...].astype(jnp.float32))
    width = columns // blocks
    for slot in range(slots):
        limits = jnp.concatenate(
            [
                jnp.broadcast_to(limit[b, :, slot : slot + 1], (sub_rows, width))
                for b in range(blocks)
            ],
            axis=1,
        )
        added = jnp.clip(delta[slot], -limits, limits).astype(jnp.bfloat16)
        sent_ref[pl.ds(owner_ref[slot_ref[slot]], 1)] = added[None]


def shards(
    master,
    first_moment,
    second_moment,
    gradient,
    scale_exponent,
    slot_expert,
    expert_owner,
    serving_weights,
):
    in_vmem = pl.BlockSpec(memory_space=pltpu.VMEM)
    in_smem = pl.BlockSpec(memory_space=pltpu.SMEM)
    sent = pl.pallas_call(
        coded_kernel,
        in_specs=[in_smem, in_smem] + [in_vmem] * 5,
        out_specs=in_vmem,
        out_shape=jax.ShapeDtypeStruct(master.shape[2:], jnp.bfloat16),
    )(
        slot_expert[0, 0],
        expert_owner,
        jnp.transpose(scale_exponent[0, 0], (2, 1, 0)),
        master[0, 0],
        first_moment[0, 0],
        second_moment[0, 0],
        gradient[0, 0],
    )
    received = lax.all_to_all(sent, "expert", split_axis=0, concat_axis=0, tiled=True)
    first_out, second_out, delta = adamw(master, first_moment, second_moment, gradient)
    master_out = master + delta
    piece = received.reshape(-1, received.shape[2])
    part = lax.all_gather(piece, "x_hi", axis=0, tiled=False)
    wire = (part.astype(jnp.float32) * LIFT).astype(jnp.float16)
    whole = lax.all_gather(wire, "z", axis=1, tiled=True)
    serving = serving_weights.reshape(whole.shape)
    added = whole.astype(jnp.float32) * (1.0 / LIFT)
    new_rows = (serving.astype(jnp.float32) + added).astype(jnp.bfloat16)
    serving_out = new_rows.reshape(serving_weights.shape)
    return (master_out, first_out, second_out, serving_out)


def solution(mesh):
    replicas, experts = mesh.devices.shape
    split = Mesh(mesh.devices.reshape(replicas // RING, RING, experts), (*REPLICA, "expert"))
    flat = P(REPLICA, "expert", None, None, None)
    served = P("expert", None, None)
    in_specs = (flat, flat, flat, flat, flat, P(REPLICA, "expert", None), P(), served)
    out_specs = (flat, flat, flat, served)
    return jax.shard_map(shards, mesh=split, in_specs=in_specs, out_specs=out_specs, check_vma=False)
```

```python
import jax
import jax.numpy as jnp
from jax import lax
from jax.experimental import pallas as pl
from jax.experimental.pallas import tpu as pltpu
from jax.sharding import Mesh
from jax.sharding import PartitionSpec as P

RING = 8
LIFT = 2.0**15
REPLICA = ("x_hi", "z")


def adamw(master, first_moment, second_moment, gradient):
    grad_full = gradient.astype(jnp.float32)
    first_out = 0.9 * first_moment + 0.1 * grad_full
    second_out = 0.95 * second_moment + 0.05 * grad_full * grad_full
    corr_first = 1.0 - 0.9**10
    corr_second = 1.0 - 0.95**10
    update = first_out / corr_first / (jnp.sqrt(second_out / corr_second) + 1e-08) + 0.1 * master
    return first_out, second_out, -0.1 * update


def coded_kernel(
    slot_ref,
    owner_ref,
    exponent_ref,
    master_ref,
    first_ref,
    second_ref,
    grad_ref,
    sent_ref,
):
    slots, sub_rows, columns = master_ref.shape
    blocks = exponent_ref.shape[0]
    _, _, delta = adamw(master_ref[...], first_ref[...], second_ref[...], grad_ref[...])
    limit = 8.0 * jnp.exp2(-exponent_ref[...].astype(jnp.float32))
    width = columns // blocks
    for slot in range(slots):
        limits = jnp.concatenate(
            [
                jnp.broadcast_to(limit[b, :, slot : slot + 1], (sub_rows, width))
                for b in range(blocks)
            ],
            axis=1,
        )
        added = jnp.clip(delta[slot], -limits, limits).astype(jnp.bfloat16)
        sent_ref[pl.ds(owner_ref[slot_ref[slot]], 1)] = added[None]


def shards(
    master,
    first_moment,
    second_moment,
    gradient,
    scale_exponent,
    slot_expert,
    expert_owner,
    serving_weights,
):
    in_vmem = pl.BlockSpec(memory_space=pltpu.VMEM)
    in_smem = pl.BlockSpec(memory_space=pltpu.SMEM)
    sent = pl.pallas_call(
        coded_kernel,
        in_specs=[in_smem, in_smem] + [in_vmem] * 5,
        out_specs=in_vmem,
        out_shape=jax.ShapeDtypeStruct(master.shape[2:], jnp.bfloat16),
    )(
        slot_expert[0, 0],
        expert_owner,
        jnp.transpose(scale_exponent[0, 0], (2, 1, 0)),
        master[0, 0],
        first_moment[0, 0],
        second_moment[0, 0],
        gradient[0, 0],
    )
    received = lax.all_to_all(sent, "expert", split_axis=0, concat_axis=0, tiled=True)
    first_out, second_out, delta = adamw(master, first_moment, second_moment, gradient)
    master_out = master + delta
    piece = received.reshape(-1, received.shape[2])
    copies = jnp.broadcast_to(piece[None], (lax.axis_size("x_hi"), *piece.shape))
    part = lax.all_to_all(copies, "x_hi", split_axis=0, concat_axis=0, tiled=True)
    wire = (part.astype(jnp.float32) * LIFT).astype(jnp.float16)
    whole = lax.all_gather(wire, "z", axis=1, tiled=True)
    serving = serving_weights.reshape(whole.shape)
    added = whole.astype(jnp.float32) * (1.0 / LIFT)
    new_rows = (serving.astype(jnp.float32) + added).astype(jnp.bfloat16)
    serving_out = new_rows.reshape(serving_weights.shape)
    return (master_out, first_out, second_out, serving_out)


def solution(mesh):
    replicas, experts = mesh.devices.shape
    split = Mesh(mesh.devices.reshape(replicas // RING, RING, experts), (*REPLICA, "expert"))
    flat = P(REPLICA, "expert", None, None, None)
    served = P("expert", None, None)
    in_specs = (flat, flat, flat, flat, flat, P(REPLICA, "expert", None), P(), served)
    out_specs = (flat, flat, flat, served)
    return jax.shard_map(shards, mesh=split, in_specs=in_specs, out_specs=out_specs, check_vma=False)
```

```python
import jax
import jax.numpy as jnp
from jax import lax
from jax.experimental import pallas as pl
from jax.experimental.pallas import tpu as pltpu
from jax.sharding import Mesh
from jax.sharding import PartitionSpec as P

RING = 8
LIFT = 2.0**15
PIECES = 8
GRANT = 8 * 2**20
REPLICA = ("x_hi", "z")


def adamw(master, first_moment, second_moment, gradient):
    grad_full = gradient.astype(jnp.float32)
    first_out = 0.9 * first_moment + 0.1 * grad_full
    second_out = 0.95 * second_moment + 0.05 * grad_full * grad_full
    corr_first = 1.0 - 0.9**10
    corr_second = 1.0 - 0.95**10
    update = first_out / corr_first / (jnp.sqrt(second_out / corr_second) + 1e-08) + 0.1 * master
    return first_out, second_out, -0.1 * update


def coded_kernel(
    slot_ref,
    owner_ref,
    exponent_ref,
    master_ref,
    first_ref,
    second_ref,
    grad_ref,
    sent_ref,
):
    slots, sub_rows, columns = master_ref.shape
    blocks = exponent_ref.shape[0]
    _, _, delta = adamw(master_ref[...], first_ref[...], second_ref[...], grad_ref[...])
    limit = 8.0 * jnp.exp2(-exponent_ref[...].astype(jnp.float32))
    width = columns // blocks
    for slot in range(slots):
        limits = jnp.concatenate(
            [
                jnp.broadcast_to(limit[b, :, slot : slot + 1], (sub_rows, width))
                for b in range(blocks)
            ],
            axis=1,
        )
        added = jnp.clip(delta[slot], -limits, limits).astype(jnp.bfloat16)
        sent_ref[pl.ds(owner_ref[slot_ref[slot]], 1)] = added[None]


def write_kernel(new_ref, out_ref, done_ref):
    step = new_ref.shape[0] // PIECES
    copies = []
    for piece in range(PIECES):
        rows = pl.ds(piece * step, step)
        copies.append(pltpu.make_async_copy(new_ref.at[rows], out_ref.at[rows], done_ref.at[piece]))
        copies[-1].start()
    for copy in copies:
        copy.wait()


def shards(
    master,
    first_moment,
    second_moment,
    gradient,
    scale_exponent,
    slot_expert,
    expert_owner,
    serving_weights,
):
    in_vmem = pl.BlockSpec(memory_space=pltpu.VMEM)
    in_smem = pl.BlockSpec(memory_space=pltpu.SMEM)
    sent = pl.pallas_call(
        coded_kernel,
        in_specs=[in_smem, in_smem] + [in_vmem] * 5,
        out_specs=in_vmem,
        out_shape=jax.ShapeDtypeStruct(master.shape[2:], jnp.bfloat16),
    )(
        slot_expert[0, 0],
        expert_owner,
        jnp.transpose(scale_exponent[0, 0], (2, 1, 0)),
        master[0, 0],
        first_moment[0, 0],
        second_moment[0, 0],
        gradient[0, 0],
    )
    received = lax.all_to_all(sent, "expert", split_axis=0, concat_axis=0, tiled=True)
    first_out, second_out, delta = adamw(master, first_moment, second_moment, gradient)
    master_out = master + delta
    piece = received.reshape(-1, received.shape[2])
    part = lax.all_gather(piece, "x_hi", axis=0, tiled=False)
    wire = (part.astype(jnp.float32) * LIFT).astype(jnp.float16)
    whole = lax.all_gather(wire, "z", axis=1, tiled=True)
    serving = serving_weights.reshape(whole.shape)
    added = whole.astype(jnp.float32) * (1.0 / LIFT)
    new_rows = (serving.astype(jnp.float32) + added).astype(jnp.bfloat16)
    new_rows = pltpu.with_memory_space_constraint(new_rows.reshape(serving_weights.shape[1:]), pltpu.VMEM)
    serving_out = pl.pallas_call(
        write_kernel,
        in_specs=[in_vmem],
        out_specs=pl.BlockSpec(memory_space=pl.ANY),
        out_shape=jax.ShapeDtypeStruct(new_rows.shape, jnp.bfloat16),
        scratch_shapes=[pltpu.SemaphoreType.DMA((PIECES,))],
        compiler_params=pltpu.CompilerParams(vmem_limit_bytes=GRANT),
    )(new_rows)[None]
    return (master_out, first_out, second_out, serving_out)


def solution(mesh):
    replicas, experts = mesh.devices.shape
    split = Mesh(mesh.devices.reshape(replicas // RING, RING, experts), (*REPLICA, "expert"))
    flat = P(REPLICA, "expert", None, None, None)
    served = P("expert", None, None)
    in_specs = (flat, flat, flat, flat, flat, P(REPLICA, "expert", None), P(), served)
    out_specs = (flat, flat, flat, served)
    return jax.shard_map(shards, mesh=split, in_specs=in_specs, out_specs=out_specs, check_vma=False)
```
